256 devices in a mesh: seq: 4 (over x), head: 4 (over y), rows: 16 (over z, core).
Axes of the slice: x: 4, y: 4, z: 8, core: 2. Of those that a mesh axis runs over, the one named last changes fastest.
Arguments:
- queries: bfloat16 [8, 4, 5120, 2048], P('seq', None, 'rows', 'head'), may hold values from -6 to 6
- keys: bfloat16 [8, 4, 5120, 2048], P('seq', None, 'rows', 'head'), may hold values from -6 to 6
- values: bfloat16 [8, 4, 5120, 2048], P('seq', None, 'rows', 'head'), may hold values from -6 to 6
- counts: int32 [8], replicated, may hold values from 1 to 4, as said below
- rate: float32 [4], P('head'), may hold values from 0.125 to 1
- w_first: bfloat16 [4, 512, 256], P('head'), may hold values from -0.25 to 0.25
- w_third: bfloat16 [4, 512, 256], P('head'), may hold values from -0.25 to 0.25
- w_second: bfloat16 [4, 256, 512], P('head'), may hold values from -0.375 to 0.375
Outputs:
- mixed: bfloat16 [8, 4, 5120, 2048], P('seq', None, 'rows', 'head')
The draws below stay inside these ranges and needn't reach their ends.
Inputs may be any that keep to these rules, and one draw needn't show every extreme that they name: `counts`: taken in order, the sequences fall into consecutive runs, as many as there are groups of 2 sequences, each run with exactly 4 blocks in all; some sequence has 4 blocks.
All inputs are finite; a program needn't handle non-finite values.
Results may differ from the reference program's by a relative error of at most 0.02.
Values may be sent and summed in bfloat16 or wider, within the bound.
No kernel may reach another device: no remote copies, remote signals or barrier semaphores. Data moves between devices by JAX's collectives and lax.ppermute only.
A program may use at most 64 MiB of HBM per device.

```python
import math
import jax
import jax.numpy as jnp
from jax import lax

D = 2048
HEADS = 4
HD = 512
FH = 256
BLOCK_DEV = 320
BLOCKS = 4
SLOTS = 2
SEQS = 8
BLOCK = 5120
N_ROWS = 16


def draw_counts(key, part):
    key = jax.random.fold_in(jax.random.fold_in(key, 7919), part)
    groups = SEQS // SLOTS
    lone_group = jax.random.randint(jax.random.fold_in(key, 11), (), 0, groups)
    group_sizes = jnp.ones((groups,), jnp.int32)
    group_ids = jnp.arange(groups, dtype=jnp.int32)
    for attempt in range(SEQS - groups):
        scores = jax.random.permutation(jax.random.fold_in(key, 100 + attempt), groups).astype(jnp.int32)
        has_room = (group_sizes < BLOCKS) & (group_ids != lone_group)
        chosen = jnp.argmax(jnp.where(has_room, scores, -1))
        group_sizes = group_sizes.at[chosen].add(1)
    run_ends = jnp.cumsum(group_sizes)
    position = jnp.arange(SEQS, dtype=jnp.int32)
    member_of = jnp.sum((position[:, None] >= run_ends[None, :]).astype(jnp.int32), axis=1)
    member = member_of[:, None] == group_ids[None, :]
    counts = jnp.ones((SEQS,), jnp.int32)
    for attempt in range(BLOCKS - 1):
        totals = jnp.sum(jnp.where(member, counts[:, None], 0), axis=0)
        scores = jax.random.permutation(jax.random.fold_in(key, 500 + attempt), SEQS).astype(jnp.int32)
        chosen = jnp.argmax(jnp.where(member, scores[:, None], -1), axis=0)
        counts = counts.at[chosen].add((totals < BLOCKS).astype(jnp.int32))
    return counts.astype(jnp.int32)


def level_of(own_key, extent, pieces, low, largest):
    def one(axis_at, parts):
        heights = jax.random.uniform(jax.random.fold_in(jax.random.fold_in(own_key, 6), axis_at), (parts,), jnp.float32, low / len(pieces), largest / len(pieces))
        return jnp.repeat(jnp.exp(heights), extent[axis_at] // parts).reshape((-1,) + (1,) * (len(extent) - axis_at - 1))

    factor_of = one(*pieces[0])
    for cut in pieces[1:]:
        factor_of = factor_of * one(*cut)
    return factor_of


def scatter_about(own_key, dims, deviation, limit, pieces=(), kind=jnp.bfloat16):
    array = jax.random.normal(own_key, dims, jnp.float32) * deviation
    if len(pieces) > 0:
        array = level_of(own_key, dims, pieces, -0.22, 0.18) * array
    return jnp.clip(array, min=-limit, max=limit).astype(kind)


def setup_inputs(seed: int = 0) -> dict:
    key_of = jax.random.split(jax.random.key(seed), 9)
    return {
        "queries": scatter_about(key_of[0], (SEQS, BLOCKS, BLOCK, D), 1.0, 6.0, ((0, 4), (2, 16), (3, 4))),
        "keys": scatter_about(key_of[1], (SEQS, BLOCKS, BLOCK, D), 1.0, 6.0, ((0, 4), (2, 16), (3, 4))),
        "values": scatter_about(key_of[2], (SEQS, BLOCKS, BLOCK, D), 1.0, 6.0, ((0, 4), (2, 16), (3, 4))),
        "counts": draw_counts(jax.random.fold_in(key_of[8], 71), 0),
        "rate": jnp.clip(jnp.exp(math.log(1.0) - 2.0794415 * jax.random.uniform(key_of[4], (HEADS,), jnp.float32) ** level_of(key_of[4], (HEADS,), ((0, 4),), -0.2, 0.2)), 0.125, 1.0),
        "w_first": scatter_about(key_of[5], (HEADS, HD, FH), HD ** -0.5, 0.25, ((0, 4),)),
        "w_third": scatter_about(key_of[6], (HEADS, HD, FH), HD ** -0.5, 0.25, ((0, 4),)),
        "w_second": scatter_about(key_of[7], (HEADS, FH, HD), FH ** -0.5, 0.375, ((0, 4),)),
    }


def normalize_rows(matrix, epsilon):
    matrix = matrix.astype(jnp.float32)
    return matrix * lax.rsqrt(lax.optimization_barrier(jnp.mean(matrix * matrix, axis=-1, keepdims=True)) + epsilon)

def column_norms(weight, axis_in):
    return jnp.sqrt(lax.optimization_barrier(jnp.sum(weight * weight, axis=axis_in)) + 1e-06)

def rescale(moved, target, axis_in):
    return moved * (jnp.expand_dims(target, axis_in) / jnp.expand_dims(column_norms(moved, axis_in), axis_in))

def rounded(matrix):
    return lax.optimization_barrier(matrix.astype(jnp.bfloat16)).astype(jnp.float32)

def block_sums(first_op, second_op):
    heads = first_op.shape[0]
    first_runs = first_op.reshape(heads, N_ROWS, BLOCK_DEV, first_op.shape[-1]).astype(jnp.float32)
    second_runs = second_op.reshape(heads, N_ROWS, BLOCK_DEV, second_op.shape[-1]).astype(jnp.float32)
    partial_sums = jnp.einsum('hnra,hnrb->hnab', first_runs, second_runs)
    return lax.optimization_barrier(jnp.sum(rounded(partial_sums), axis=1))

def reference(queries, keys, values, counts, rate, w_first, w_third, w_second):
    heads, head_width, hidden_units = w_first.shape
    start_weights = (w_first.astype(jnp.float32), w_third.astype(jnp.float32), w_second.astype(jnp.float32))
    targets = tuple((column_norms(weight, 1) for weight in start_weights))
    step_rate = (rate / BLOCK)[:, None, None]

    def split_heads(block_rows):
        return block_rows.reshape(BLOCK, heads, head_width).transpose(1, 0, 2)

    def one_sequence(inputs):
        seq_queries, seq_keys, seq_values, length = inputs

        def advance(master, step_inputs):
            query_rows, key_rows, value_rows, block_index = step_inputs
            is_live = block_index < length
            current = tuple((rounded(weight) for weight in master))
            key_norm = normalize_rows(split_heads(key_rows), 1e-06).astype(jnp.bfloat16)
            key_float = key_norm.astype(jnp.float32)
            gate_pre = jnp.einsum('hrd,hdf->hrf', key_float, current[0])
            up_pre = jnp.einsum('hrd,hdf->hrf', key_float, current[1])
            gate_sig = jax.nn.sigmoid(gate_pre)
            gate_act = gate_pre * gate_sig
            hidden = (gate_act * up_pre).astype(jnp.bfloat16)
            value_heads = split_heads(value_rows)
            d_hidden = jnp.einsum('hrd,hfd->hrf', value_heads.astype(jnp.float32), current[2])
            d_gate = (d_hidden * up_pre * gate_sig * (1.0 + gate_pre * (1.0 - gate_sig))).astype(jnp.bfloat16)
            d_up = (d_hidden * gate_act).astype(jnp.bfloat16)
            sums = (block_sums(key_norm, d_gate), block_sums(key_norm, d_up), block_sums(hidden, value_heads))
            moved = tuple((rescale(weight + step_rate * grad_total, target, 1) for weight, grad_total, target in zip(master, sums, targets)))
            master = tuple((jnp.where(is_live, new_w, old_w) for new_w, old_w in zip(moved, master)))
            current = tuple((rounded(weight) for weight in master))
            query_float = rounded(normalize_rows(split_heads(query_rows), 1e-06))
            out_gate = jnp.einsum('hrd,hdf->hrf', query_float, current[0])
            out_up = jnp.einsum('hrd,hdf->hrf', query_float, current[1])
            out_hidden = rounded(out_gate * jax.nn.sigmoid(out_gate) * out_up)
            output = jnp.einsum('hrf,hfd->hrd', out_hidden, current[2])
            output = normalize_rows(output, 1e-05).astype(jnp.bfloat16)
            merged = output.transpose(1, 0, 2).reshape(BLOCK, heads * head_width)
            return (master, jnp.where(is_live, merged, jnp.zeros_like(merged)))
        block_ids = jnp.arange(BLOCKS, dtype=jnp.int32)
        _, outputs = lax.scan(advance, start_weights, (seq_queries, seq_keys, seq_values, block_ids))
        return outputs
    return lax.map(one_sequence, (queries, keys, values, counts))
```

```python
import jax
import jax.numpy as jnp
from jax import lax
from jax.experimental import pallas as pl
from jax.experimental.pallas import tpu as pltpu
from jax.sharding import Mesh, PartitionSpec as P

F32 = jnp.float32
BF16 = jnp.bfloat16
NT = (((1,), (1,)), ((), ()))
NN = (((1,), (0,)), ((), ()))
TN = (((0,), (0,)), ((), ()))


def dot(first_op, second_op, dims):
    return lax.dot_general(first_op, second_op, dims, preferred_element_type=F32)


def normalized(rows, epsilon):
    rows = rows.astype(F32)
    return rows * lax.rsqrt(jnp.mean(rows * rows, axis=-1, keepdims=True) + epsilon)


def weights_of(w_ref, target_ref):
    hidden = w_ref.shape[0] * w_ref.shape[2]
    parts = [w_ref[:, i].reshape(hidden, w_ref.shape[3]) for i in range(3)]
    down = parts[2].astype(F32)
    scale = target_ref[...] / jnp.sqrt(jnp.sum(down * down, axis=0, keepdims=True) + 1e-06)
    return parts[0], parts[1], (down * scale).astype(BF16), scale


def sums_kernel(info, k_ref, v_ref, w_ref, w0_ref, target_ref, own_ref, send_ref, scale_ref, pick_ref):
    restart, core = info[1], info[2]

    @pl.when(restart == 1)
    def _():
        pick_ref[...] = w0_ref[...]

    @pl.when(restart == 0)
    def _():
        pick_ref[...] = w_ref[...]

    gate, up, down, scale = weights_of(pick_ref, target_ref)
    scale_ref[...] = scale
    keys = normalized(k_ref[0], 1e-06).astype(BF16)
    values = v_ref[0]
    gate_pre = dot(keys, gate, NT)
    up_pre = dot(keys, up, NT)
    d_hidden = dot(values, down, NT)
    gate_sig = jax.nn.sigmoid(gate_pre)
    gate_act = gate_pre * gate_sig
    hidden = (gate_act * up_pre).astype(BF16)
    d_gate = (d_hidden * up_pre * gate_sig * (1.0 + gate_pre * (1.0 - gate_sig))).astype(BF16)
    d_up = (d_hidden * gate_act).astype(BF16)
    n, _, rows, width = own_ref.shape
    for i, (left, right) in enumerate(((d_gate, keys), (d_up, keys), (hidden, values))):
        total = dot(left, right, TN).astype(BF16).reshape(n, 2, rows, width)

        @pl.when(core == 0)
        def _():
            own_ref[:, i] = total[:, 0]
            send_ref[:, i] = total[:, 1]

        @pl.when(core == 1)
        def _():
            own_ref[:, i] = total[:, 1]
            send_ref[:, i] = total[:, 0]


def update_kernel(info, step_ref, x_ref, m_ref, m0_ref, scale_ref, goal_ref, w_ref, out_ref):
    keep = info[0] == 0
    total = jnp.sum(x_ref[...].astype(F32), axis=0) * step_ref[0]
    for i in range(3):
        old = jnp.where(keep, m_ref[i], m0_ref[i])
        if i == 2:
            new = old * scale_ref[...] + total[i]
        else:
            moved = old + total[i]
            norm = jnp.sqrt(jnp.sum(moved * moved, axis=1, keepdims=True) + 1e-06)
            new = moved * (goal_ref[i] / norm)
        out_ref[i] = new
        w_ref[i] = new.astype(BF16)


def answer_kernel(info, q_ref, w_ref, target_ref, old_ref, out_ref):
    @pl.when(info[1] == 1)
    def _():
        gate, up, down, _ = weights_of(w_ref, target_ref)
        query = normalized(q_ref[0], 1e-06).astype(BF16)
        out_gate = dot(query, gate, NT)
        out_up = dot(query, up, NT)
        out_hidden = (out_gate * jax.nn.sigmoid(out_gate) * out_up).astype(BF16)
        out_ref[0] = normalized(dot(out_hidden, down, NN), 1e-05).astype(BF16)

    @pl.when(info[1] == 0)
    def _():
        out_ref[0] = jnp.zeros_like(out_ref[0])


def call(kernel, n_scalars, in_specs, out_specs, out_shape, scratch=(), **kw):
    return pl.pallas_call(
        kernel,
        grid_spec=pltpu.PrefetchScalarGridSpec(
            num_scalar_prefetch=n_scalars, grid=(1,), in_specs=in_specs, out_specs=out_specs, scratch_shapes=scratch
        ),
        out_shape=out_shape,
        compiler_params=pltpu.CompilerParams(vmem_limit_bytes=48 << 20),
        **kw,
    )


def whole(shape):
    return pl.BlockSpec(shape, lambda *_: (0,) * len(shape))


def body(queries, keys, values, counts, rate, w_first, w_third, w_second):
    slots, blocks, block_rows, width = queries.shape
    hidden = w_first.shape[2]
    n_z, n_core = lax.axis_size("z"), lax.axis_size("core")
    n_dev = n_z * n_core
    share = hidden // n_dev
    group, core = lax.axis_index("seq"), lax.axis_index("core")
    me = lax.axis_index("z") * n_core + core
    step = (rate / (block_rows * n_dev)).astype(F32)

    flat = (slots * blocks, block_rows, width)
    queries, keys, values = (a.reshape(flat) for a in (queries, keys, values))
    start = jnp.stack([w_first[0].T, w_third[0].T, w_second[0]])
    w0 = start.reshape(3, n_dev, share, width).transpose(1, 0, 2, 3)
    m0 = lax.dynamic_index_in_dim(w0, me, 0, keepdims=False).astype(F32)
    goal = jnp.sqrt(jnp.sum(m0[:2] * m0[:2], axis=2, keepdims=True) + 1e-06)
    second = w_second[0].astype(F32)
    target = jnp.sqrt(jnp.sum(second * second, axis=0, keepdims=True) + 1e-06)

    local = lax.dynamic_slice_in_dim(counts, group * slots, slots)
    first_len, live = local[0], local[0] + local[1]

    def place(t):
        return jnp.where(t < first_len, t, blocks + t - first_len)

    w_shape, m_shape = (n_dev, 3, share, width), (3, share, width)
    half = (n_z, 3, share, width)
    row_block = lambda: pl.BlockSpec((1, block_rows, width), lambda i, info: (info[0], 0, 0))

    def sums(t, w):
        t = jnp.minimum(t, live - 1)
        restart = ((t == 0) | (t == first_len)).astype(jnp.int32)
        info = jnp.stack([place(t), restart, core])
        return call(
            sums_kernel,
            1,
            [row_block(), row_block(), whole(w_shape), whole(w_shape), whole((1, width))],
            [whole(half), whole(half), whole((1, width))],
            [jax.ShapeDtypeStruct(half, BF16), jax.ShapeDtypeStruct(half, BF16), jax.ShapeDtypeStruct((1, width), F32)],
            [pltpu.VMEM(w_shape, BF16)],
        )(info, keys, values, w, w0, target)

    def update(t, x, m, scale):
        restart = ((t == 0) | (t == first_len)).astype(jnp.int32)
        return call(
            update_kernel,
            2,
            [whole(half), whole(m_shape), whole(m_shape), whole((1, width)), whole(goal.shape)],
            [whole(m_shape), whole(m_shape)],
            [jax.ShapeDtypeStruct(m_shape, BF16), jax.ShapeDtypeStruct(m_shape, F32)],
        )(restart[None], step, x, m, m0, scale, goal)

    def answer(t, on, w, out):
        info = jnp.stack([place(t), on.astype(jnp.int32)])
        return call(
            answer_kernel,
            1,
            [row_block(), whole(w_shape), whole((1, width)), pl.BlockSpec(memory_space=pl.ANY)],
            row_block(),
            jax.ShapeDtypeStruct(flat, BF16),
            input_output_aliases={4: 0},
        )(info, queries, w, target, out)

    def advance(t, carry):
        own, send, scale, w, m, out = carry
        got = lax.ppermute(send, "core", [(0, 1), (1, 0)])
        out = answer(jnp.maximum(t - 1, 0), t > 0, w, out)
        pair = (own.astype(F32) + got.astype(F32)).astype(BF16)
        parts = lax.all_to_all(pair, "z", 0, 0, tiled=True)
        chunk, m = update(t, parts, m, scale)
        w = lax.all_gather(chunk, ("z", "core"), axis=0)
        own, send, scale = sums(t + 1, w)
        return own, send, scale, w, m, out

    out = jnp.zeros(flat, BF16)
    own, send, scale = sums(jnp.int32(0), w0)
    carry = lax.fori_loop(0, live, advance, (own, send, scale, w0, m0, out))
    out = answer(live - 1, live > 0, carry[3], carry[5])
    return out.reshape(slots, blocks, block_rows, width)


def solution(mesh):
    seq, head, rows = (mesh.shape[name] for name in ("seq", "head", "rows"))
    split = Mesh(mesh.devices.reshape(seq, head, rows // 2, 2), ("seq", "head", "z", "core"))
    data = P("seq", None, ("z", "core"), "head")
    weight = P("head", None, None)
    return jax.shard_map(
        body,
        mesh=split,
        in_specs=(data, data, data, P(), P("head"), weight, weight, weight),
        out_specs=data,
        check_vma=False,
    )
```

```python
import functools

import jax
import jax.numpy as jnp
from jax import lax
from jax.experimental import pallas as pl
from jax.experimental.pallas import tpu as pltpu
from jax.sharding import Mesh, PartitionSpec as P


F32 = jnp.float32
BF16 = jnp.bfloat16
NT = (((1,), (1,)), ((), ()))
NN = (((1,), (0,)), ((), ()))
TN = (((0,), (0,)), ((), ()))


def dot(first_op, second_op, dims):
    return lax.dot_general(first_op, second_op, dims, preferred_element_type=F32)


def normalized(rows, epsilon):
    rows = rows.astype(F32)
    return rows * lax.rsqrt(jnp.mean(rows * rows, axis=-1, keepdims=True) + epsilon)


def weights_of(w_ref, target_ref):
    parts = [w_ref[:, i].reshape(-1, w_ref.shape[3]) for i in range(3)]
    down = parts[2].astype(F32)
    scale = target_ref[...] / jnp.sqrt(jnp.sum(down * down, axis=0, keepdims=True) + 1e-06)
    return parts[0], parts[1], (down * scale).astype(BF16), scale


def init_kernel(counts, gate_ref, up_ref, down_ref, w_ref, chunk_ref, m_ref, goal_ref, target_ref, meta_ref, *, blocks, slots):
    core = lax.axis_index("core")
    me = lax.axis_index("z") * lax.axis_size("core") + core
    first = lax.axis_index("seq") * slots
    n_first, n_second = counts[first], counts[first + 1]
    second_longer = n_second > n_first
    meta_ref[0] = jnp.where(second_longer, blocks, 0)
    meta_ref[1] = jnp.maximum(n_first, n_second)
    meta_ref[2] = jnp.where(second_longer, 0, blocks)
    meta_ref[3] = jnp.minimum(n_first, n_second)
    meta_ref[4] = core
    n_dev, _, share, width = w_ref.shape
    down = down_ref[0]
    for i, part in enumerate((gate_ref[0].astype(F32).T.astype(BF16), up_ref[0].astype(F32).T.astype(BF16), down)):
        w_ref[:, i] = part.reshape(n_dev, share, width)
    down = down.astype(F32)
    target_ref[...] = jnp.sqrt(jnp.sum(down * down, axis=0, keepdims=True) + 1e-06)
    mine = w_ref[me]
    chunk_ref[...] = mine
    mine = mine.astype(F32)
    m_ref[...] = mine
    for i in range(2):
        goal_ref[i] = jnp.sqrt(jnp.sum(mine[i] * mine[i], axis=1, keepdims=True) + 1e-06)


def sums_kernel(t, meta, k_ref, v_ref, w_ref, target_ref, keep_ref, send_ref, scale_ref):
    core = meta[4]
    gate, up, down, scale = weights_of(w_ref, target_ref)
    scale_ref[...] = scale
    keys = normalized(k_ref[0], 1e-06).astype(BF16)
    values = v_ref[0]
    gate_pre = dot(keys, gate, NT)
    up_pre = dot(keys, up, NT)
    d_hidden = dot(values, down, NT)
    gate_sig = jax.nn.sigmoid(gate_pre)
    gate_act = gate_pre * gate_sig
    hidden = (gate_act * up_pre).astype(BF16)
    d_gate = (d_hidden * up_pre * gate_sig * (1.0 + gate_pre * (1.0 - gate_sig))).astype(BF16)
    d_up = (d_hidden * gate_act).astype(BF16)
    n, _, rows, width = keep_ref.shape
    for i, (left, right) in enumerate(((d_gate, keys), (d_up, keys), (hidden, values))):
        total = dot(left, right, TN).astype(BF16).reshape(n, 2, rows, width)

        @pl.when(core == 0)
        def _():
            keep_ref[:, i] = total[:, 0]
            send_ref[:, i] = total[:, 1]

        @pl.when(core == 1)
        def _():
            keep_ref[:, i] = total[:, 1]
            send_ref[:, i] = total[:, 0]


def update_kernel(step_ref, x_ref, m_ref, scale_ref, goal_ref, w_ref, out_ref):
    total = jnp.sum(x_ref[...].astype(F32), axis=0) * step_ref[0]
    for i in range(3):
        if i == 2:
            new = m_ref[i] * scale_ref[...] + total[i]
        else:
            moved = m_ref[i] + total[i]
            norm = jnp.sqrt(jnp.sum(moved * moved, axis=1, keepdims=True) + 1e-06)
            new = moved * (goal_ref[i] / norm)
        out_ref[i] = new
        w_ref[i] = new.astype(BF16)


def answer_kernel(t, meta, q_ref, w_ref, target_ref, old_ref, out_ref, *, chain, shift):
    at = t[0] - shift
    live = (at >= 0) & (at < meta[2 * chain + 1])

    @pl.when(live)
    def _():
        gate, up, down, _ = weights_of(w_ref, target_ref)
        query = normalized(q_ref[0], 1e-06).astype(BF16)
        out_gate = dot(query, gate, NT)
        out_up = dot(query, up, NT)
        out_hidden = (out_gate * jax.nn.sigmoid(out_gate) * out_up).astype(BF16)
        out_ref[0] = normalized(dot(out_hidden, down, NN), 1e-05).astype(BF16)

    @pl.when(jnp.logical_not(live))
    def _():
        out_ref[0] = jnp.zeros_like(out_ref[0])


def call(kernel, n_scalars, in_specs, out_specs, out_shape, cost=None, **kw):
    return pl.pallas_call(
        kernel,
        grid_spec=pltpu.PrefetchScalarGridSpec(
            num_scalar_prefetch=n_scalars, grid=(1,), in_specs=in_specs, out_specs=out_specs
        ),
        out_shape=out_shape,
        compiler_params=pltpu.CompilerParams(vmem_limit_bytes=40 << 20),
        cost_estimate=cost,
        **kw,
    )


def whole(shape):
    return pl.BlockSpec(shape, lambda *_: (0,) * len(shape))


def body(queries, keys, values, counts, rate, w_first, w_third, w_second):
    slots, blocks, block_rows, width = queries.shape
    hidden = w_first.shape[2]
    n_z, n_core = lax.axis_size("z"), lax.axis_size("core")
    n_dev = n_z * n_core
    share = hidden // n_dev
    step = (rate / (block_rows * n_dev)).astype(F32)
    flat = (slots * blocks, block_rows, width)
    queries, keys, values = (a.reshape(flat) for a in (queries, keys, values))
    w_shape, half, m_shape = (n_dev, 3, share, width), (n_z, 3, share, width), (3, share, width)
    goal_shape, line = (2, share, 1), (1, width)
    shape = jax.ShapeDtypeStruct
    heavy = pl.CostEstimate(flops=2 * 3 * 2 * block_rows * width * hidden, transcendentals=0, bytes_accessed=6 << 20)

    w_init, chunk, m_init, goal, target, meta = call(
        functools.partial(init_kernel, blocks=blocks, slots=slots),
        1,
        [whole((1, width, hidden)), whole((1, width, hidden)), whole((1, hidden, width))],
        [whole(w_shape), whole(m_shape), whole(m_shape), whole(goal_shape), whole(line), pl.BlockSpec(memory_space=pltpu.SMEM)],
        [shape(w_shape, BF16), shape(m_shape, BF16), shape(m_shape, F32), shape(goal_shape, F32), shape(line, F32), shape((8,), jnp.int32)],
    )(counts, w_first, w_third, w_second)
    longest, shortest = meta[1], meta[3]

    def row_block(chain, shift):
        index = lambda i, t, meta: (meta[2 * chain] + jnp.clip(t[0] - shift, 0, blocks - 1), 0, 0)
        return pl.BlockSpec((1, block_rows, width), index)

    def sums(chain, t, shift, w):
        keep, send, scale = call(
            sums_kernel,
            2,
            [row_block(chain, shift), row_block(chain, shift), whole(w_shape), whole(line)],
            [whole(half), whole(half), whole(line)],
            [shape(half, BF16), shape(half, BF16), shape(line, F32)],
            heavy,
        )(t, meta, keys, values, w, target)
        got = lax.ppermute(send, "core", [(0, 1), (1, 0)])
        return (keep.astype(F32) + got.astype(F32)).astype(BF16), scale

    def reduce(pair):
        return lax.all_to_all(pair, "z", 0, 0, tiled=True)

    def update(x, m, scale):
        return call(
            update_kernel,
            1,
            [whole(half), whole(m_shape), whole(line), whole(goal_shape)],
            [whole(m_shape), whole(m_shape)],
            [shape(m_shape, BF16), shape(m_shape, F32)],
        )(step, x, m, scale, goal)

    def gather(chunk):
        return lax.all_gather(chunk, ("z", "core"), axis=0)

    def answer(chain, t, shift, w, out):
        return call(
            functools.partial(answer_kernel, chain=chain, shift=shift),
            2,
            [row_block(chain, shift), whole(w_shape), whole(line), pl.BlockSpec(memory_space=pl.ANY)],
            row_block(chain, shift),
            shape(flat, BF16),
            heavy,
            input_output_aliases={5: 0},
        )(t, meta, queries, w, target, out)

    def both(i, carry):
        chunk0, m0, pair1, scale1, m1, out = carry
        t = jnp.reshape(i, (1,))
        got1 = reduce(pair1)
        w0 = gather(chunk0)
        pair0, scale0 = sums(0, t, 0, w0)
        out = answer(0, t, 1, w0, out)
        got1, pair0 = lax.optimization_barrier((got1, pair0))
        chunk1, m1 = update(got1, m1, scale1)
        got0 = reduce(pair0)
        w1 = gather(chunk1)
        pair1, scale1 = sums(1, t, -1, w1)
        out = answer(1, t, 0, w1, out)
        chunk0, m0 = update(got0, m0, scale0)
        return chunk0, m0, pair1, scale1, m1, out

    def one(i, carry):
        chunk, m, out = carry
        t = jnp.reshape(i, (1,))
        w = gather(chunk)
        pair, scale = sums(0, t, 0, w)
        got = reduce(pair)
        out = answer(0, t, 1, w, out)
        chunk, m = update(got, m, scale)
        return chunk, m, out

    out = jnp.zeros(flat, BF16)
    pair1, scale1 = sums(1, jnp.zeros((1,), jnp.int32), 0, w_init)
    chunk0, m0, _, _, _, out = lax.fori_loop(0, shortest, both, (chunk, m_init, pair1, scale1, m_init, out))
    chunk0, _, out = lax.fori_loop(shortest, longest, one, (chunk0, m0, out))
    out = answer(0, jnp.reshape(longest, (1,)), 1, gather(chunk0), out)
    return out.reshape(slots, blocks, block_rows, width)


def solution(mesh):
    seq, head, rows = (mesh.shape[name] for name in ("seq", "head", "rows"))
    split = Mesh(mesh.devices.reshape(seq, head, rows // 2, 2), ("seq", "head", "z", "core"))
    data = P("seq", None, ("z", "core"), "head")
    weight = P("head", None, None)
    return jax.shard_map(
        body,
        mesh=split,
        in_specs=(data, data, data, P(), P("head"), weight, weight, weight),
        out_specs=data,
        check_vma=False,
    )
```

```python
import functools

import jax
import jax.numpy as jnp
from jax import lax
from jax.experimental import pallas as pl
from jax.experimental.pallas import tpu as pltpu
from jax.sharding import Mesh, PartitionSpec as P

F32 = jnp.float32
BF16 = jnp.bfloat16
NT = (((1,), (1,)), ((), ()))
NN = (((1,), (0,)), ((), ()))
TN = (((0,), (0,)), ((), ()))


def dot(first_op, second_op, dims):
    return lax.dot_general(first_op, second_op, dims, preferred_element_type=F32)


def normalized(rows, epsilon):
    rows = rows.astype(F32)
    return rows * lax.rsqrt(jnp.mean(rows * rows, axis=-1, keepdims=True) + epsilon)


def weights_of(w_ref, target_ref):
    parts = [w_ref[:, i].reshape(-1, w_ref.shape[3]) for i in range(3)]
    down = parts[2].astype(F32)
    scale = target_ref[...] / jnp.sqrt(jnp.sum(down * down, axis=0, keepdims=True) + 1e-06)
    return parts[0], parts[1], (down * scale).astype(BF16), scale


SOURCE, OWN, RESTART, HIGH, LOW, DEAD, CORE, KEPT = 0, 4, 8, 12, 16, 20, 28, 32
PLAN = 40


def copy_all(pairs, sem):
    copies = [pltpu.make_async_copy(a, b, sem.at[i]) for i, (a, b) in enumerate(pairs)]
    for c in copies:
        c.start()
    return copies


def plan_kernel(counts, k_ref, v_ref, plan, up_ref, down_ref, sem, *, run, slots, blocks):
    group = lax.axis_index("seq")
    n = lax.axis_size("seq") * slots
    ends, total = [], 0
    for s in range(n):
        total = total + counts[s]
        ends.append(total)

    def find(b):
        seq, start = jnp.int32(0), jnp.int32(0)
        for end in ends:
            passed = end <= b
            seq = seq + passed.astype(jnp.int32)
            start = jnp.where(passed, end, start)
        return seq, b - start

    for p in range(run):
        seq, block = find(group * run + p)
        owner = seq // slots
        flat = jnp.clip((seq - owner * slots) * blocks + block, 0, slots * blocks - 1)
        plan[SOURCE + p] = jnp.clip(owner - group + 1, 0, 2)
        plan[OWN + p] = flat
        plan[RESTART + p] = (block == 0).astype(jnp.int32)
        plan[KEPT + p] = jnp.where(owner == group, flat, -1)
        for place, other in ((HIGH, group + 1), (LOW, group - 1)):
            b = other * run + p
            seq, block = find(b)
            flat = jnp.clip((seq - group * slots) * blocks + block, 0, slots * blocks - 1)
            plan[place + p] = jnp.where((b >= 0) & (seq // slots == group), flat, -1)
    for i in range(slots * blocks):
        plan[DEAD + i] = (i % blocks >= counts[group * slots + i // blocks]).astype(jnp.int32)
    plan[CORE] = lax.axis_index("core")
    high, low = jnp.maximum(plan[HIGH], 0), jnp.maximum(plan[LOW], 0)
    pairs = [(k_ref.at[high], up_ref.at[0]), (v_ref.at[high], up_ref.at[1])]
    pairs += [(k_ref.at[low], down_ref.at[0]), (v_ref.at[low], down_ref.at[1])]
    for c in copy_all(pairs, sem):
        c.wait()


def pack_kernel(plan, q_ref, k_ref, v_ref, *refs, wanted):
    sem, outs = refs[-1], refs[:-1]
    pairs = []
    for j, batch in enumerate(wanted):
        for side, place in enumerate((HIGH, LOW)):
            for i, (name, p) in enumerate(batch):
                source = {"q": q_ref, "k": k_ref, "v": v_ref}[name]
                pairs.append((source.at[jnp.maximum(plan[place + p], 0)], outs[2 * j + side].at[i]))
    for c in copy_all(pairs, sem):
        c.wait()


def fetch(plan, p, wanted, sem):
    for s in range(3):

        @pl.when(plan[SOURCE + p] == s)
        def _():
            for i, (local, up, down, at, target) in enumerate(wanted):
                source = (up.at[at], local.at[plan[OWN + p]], down.at[at])[s]
                pltpu.make_async_copy(source, target, sem.at[i]).start()

    return [pltpu.make_async_copy(w[0].at[0], w[4], sem.at[i]) for i, w in enumerate(wanted)]


def init_kernel(gate_hbm, up_hbm, down_hbm, w_ref, m_ref, goal_ref, target_ref, gate_ref, up_ref, down_ref, sem):
    me = lax.axis_index("z") * lax.axis_size("core") + lax.axis_index("core")
    for c in copy_all([(gate_hbm.at[0], gate_ref), (up_hbm.at[0], up_ref), (down_hbm.at[0], down_ref)], sem):
        c.wait()
    n_dev, _, share, width = w_ref.shape
    down = down_ref[...]
    for i, part in enumerate((gate_ref[...].astype(F32).T.astype(BF16), up_ref[...].astype(F32).T.astype(BF16), down)):
        w_ref[:, i] = part.reshape(n_dev, share, width)
    down = down.astype(F32)
    target_ref[...] = jnp.sqrt(jnp.sum(down * down, axis=0, keepdims=True) + 1e-06)
    mine = w_ref[me].astype(F32)
    m_ref[...] = mine
    for i in range(2):
        goal_ref[i] = jnp.sqrt(jnp.sum(mine[i] * mine[i], axis=1, keepdims=True) + 1e-06)


def sums_kernel(plan, k_hbm, v_hbm, up_hbm, down_hbm, w_ref, w0_ref, target_ref, keep_ref, send_ref, scale_ref, k_ref, v_ref, sem, *, p, at):
    copies = fetch(plan, p, [(k_hbm, up_hbm, down_hbm, at, k_ref), (v_hbm, up_hbm, down_hbm, at + 1, v_ref)], sem)
    core = plan[CORE]
    w = jnp.where(plan[RESTART + p] == 1, w0_ref[...], w_ref[...])
    gate, up, down, scale = weights_of(w, target_ref)
    scale_ref[...] = scale
    for c in copies:
        c.wait()
    keys = normalized(k_ref[...], 1e-06).astype(BF16)
    values = v_ref[...]
    gate_pre = dot(keys, gate, NT)
    up_pre = dot(keys, up, NT)
    d_hidden = dot(values, down, NT)
    gate_sig = jax.nn.sigmoid(gate_pre)
    gate_act = gate_pre * gate_sig
    hidden = (gate_act * up_pre).astype(BF16)
    d_gate = (d_hidden * up_pre * gate_sig * (1.0 + gate_pre * (1.0 - gate_sig))).astype(BF16)
    d_up = (d_hidden * gate_act).astype(BF16)
    n, _, rows, width = keep_ref.shape
    for i, (left, right) in enumerate(((d_gate, keys), (d_up, keys), (hidden, values))):
        total = dot(left, right, TN).astype(BF16).reshape(n, 2, rows, width)

        @pl.when(core == 0)
        def _():
            keep_ref[:, i] = total[:, 0]
            send_ref[:, i] = total[:, 1]

        @pl.when(core == 1)
        def _():
            keep_ref[:, i] = total[:, 1]
            send_ref[:, i] = total[:, 0]


def update_kernel(plan, step_ref, x_ref, m_ref, m0_ref, scale_ref, goal_ref, w_ref, out_ref, *, p):
    restart = plan[RESTART + p] == 1
    total = jnp.sum(x_ref[...].astype(F32), axis=0) * step_ref[0]
    for i in range(3):
        old = jnp.where(restart, m0_ref[i], m_ref[i])
        if i == 2:
            new = old * scale_ref[...] + total[i]
        else:
            moved = old + total[i]
            norm = jnp.sqrt(jnp.sum(moved * moved, axis=1, keepdims=True) + 1e-06)
            new = moved * (goal_ref[i] / norm)
        out_ref[i] = new
        w_ref[i] = new.astype(BF16)


def answer_kernel(plan, q_hbm, up_hbm, down_hbm, w_ref, target_ref, out_ref, q_ref, sem, *, p, at):
    copies = fetch(plan, p, [(q_hbm, up_hbm, down_hbm, at, q_ref)], sem)
    gate, up, down, _ = weights_of(w_ref, target_ref)
    for c in copies:
        c.wait()
    query = normalized(q_ref[...], 1e-06).astype(BF16)
    out_gate = dot(query, gate, NT)
    out_up = dot(query, up, NT)
    out_hidden = (out_gate * jax.nn.sigmoid(out_gate) * out_up).astype(BF16)
    out_ref[...] = normalized(dot(out_hidden, down, NN), 1e-05).astype(BF16)


def place_kernel(plan, *refs, positions, fill):
    n = 3 * len(positions)
    old, out_ref, zero_ref, sem = refs[n:]
    moves = []
    for j, p in enumerate(positions):
        for i, place in enumerate((KEPT, LOW, HIGH)):
            moves.append((plan[place + p] >= 0, refs[3 * j + i], jnp.maximum(plan[place + p], 0)))
    if fill:
        zero_ref[...] = jnp.zeros_like(zero_ref)
        moves += [(plan[DEAD + i] == 1, zero_ref, i) for i in range(out_ref.shape[0])]
    copies = [(on, pltpu.make_async_copy(source, out_ref.at[i], sem.at[k])) for k, (on, source, i) in enumerate(moves)]
    for on, c in copies:
        pl.when(on)(c.start)
    for on, c in copies:
        pl.when(on)(c.wait)


def call(kernel, n_scalars, in_specs, out_specs, out_shape, scratch=(), cost=None, **kw):
    return pl.pallas_call(
        kernel,
        grid_spec=pltpu.PrefetchScalarGridSpec(
            num_scalar_prefetch=n_scalars, grid=(1,), in_specs=in_specs, out_specs=out_specs, scratch_shapes=scratch
        ),
        out_shape=out_shape,
        compiler_params=pltpu.CompilerParams(vmem_limit_bytes=16 << 20),
        cost_estimate=cost,
        **kw,
    )


def whole(shape):
    return pl.BlockSpec(shape, lambda *_: (0,) * len(shape))


ANY = pl.BlockSpec(memory_space=pl.ANY)
HBM = pl.BlockSpec(memory_space=pltpu.HBM)


def body(queries, keys, values, counts, rate, w_first, w_third, w_second):
    slots, blocks, block_rows, width = queries.shape
    hidden = w_first.shape[2]
    n_z, n_core, n_seq = lax.axis_size("z"), lax.axis_size("core"), lax.axis_size("seq")
    n_dev = n_z * n_core
    share = hidden // n_dev
    run = blocks
    step = (rate / (block_rows * n_dev)).astype(F32)
    rows = (block_rows, width)
    flat = (slots * blocks, *rows)
    far = lambda a: pltpu.with_memory_space_constraint(a, pltpu.HBM)
    queries, keys, values = (far(a.reshape(flat)) for a in (queries, keys, values))
    w_shape, half, m_shape = (n_dev, 3, share, width), (n_z, 3, share, width), (3, share, width)
    goal_shape, line = (2, share, 1), (1, width)
    shape = jax.ShapeDtypeStruct
    dma = pltpu.SemaphoreType.DMA
    heavy = pl.CostEstimate(flops=2 * 3 * 2 * block_rows * width * hidden, transcendentals=0, bytes_accessed=6 << 20)

    def both_ways(up, down):
        upward = [(i, i + 1) for i in range(n_seq - 1)]
        return lax.ppermute(up, "seq", upward), lax.ppermute(down, "seq", [(b, a) for a, b in upward])

    def batch_shape(n):
        return pltpu.HBM((n, *rows), BF16)

    plan, up, down = call(
        functools.partial(plan_kernel, run=run, slots=slots, blocks=blocks),
        1,
        [HBM, HBM],
        [pl.BlockSpec(memory_space=pltpu.SMEM), HBM, HBM],
        [shape((PLAN,), jnp.int32), batch_shape(2), batch_shape(2)],
        [dma((4,))],
    )(counts, keys, values)
    got = both_ways(up, down)

    wanted = [[("q", p - 1), ("k", p), ("v", p)] for p in range(1, run)]
    wanted[-1].append(("q", run - 1))
    sizes = [len(b) for b in wanted for _ in range(2)]
    packed = call(
        functools.partial(pack_kernel, wanted=wanted),
        1,
        [HBM, HBM, HBM],
        [HBM] * len(sizes),
        [batch_shape(n) for n in sizes],
        [dma((sum(sizes),))],
    )(plan, queries, keys, values)

    w0, m0, goal, target = call(
        init_kernel,
        0,
        [HBM, HBM, HBM],
        [whole(w_shape), whole(m_shape), whole(goal_shape), whole(line)],
        [shape(w_shape, BF16), shape(m_shape, F32), shape(goal_shape, F32), shape(line, F32)],
        [pltpu.VMEM((width, hidden), BF16), pltpu.VMEM((width, hidden), BF16), pltpu.VMEM((hidden, width), BF16), dma((3,))],
    )(w_first, w_third, w_second)

    def sums(p, got, at, w):
        keep, send, scale = call(
            functools.partial(sums_kernel, p=p, at=at),
            1,
            [HBM, HBM, ANY, ANY, whole(w_shape), whole(w_shape), whole(line)],
            [whole(half), whole(half), whole(line)],
            [shape(half, BF16), shape(half, BF16), shape(line, F32)],
            [pltpu.VMEM(rows, BF16), pltpu.VMEM(rows, BF16), dma((2,))],
            heavy,
        )(plan, keys, values, *got, w, w0, target)
        other = lax.ppermute(send, "core", [(0, 1), (1, 0)])
        return (keep.astype(F32) + other.astype(F32)).astype(BF16), scale

    def update(p, x, m, scale):
        return call(
            functools.partial(update_kernel, p=p),
            2,
            [whole(half), whole(m_shape), whole(m_shape), whole(line), whole(goal_shape)],
            [whole(m_shape), whole(m_shape)],
            [shape(m_shape, BF16), shape(m_shape, F32)],
        )(plan, step, x, m, m0, scale, goal)

    def answer(p, got, at, w):
        return call(
            functools.partial(answer_kernel, p=p, at=at),
            1,
            [HBM, ANY, ANY, whole(w_shape), whole(line)],
            whole(rows),
            shape(rows, BF16),
            [pltpu.VMEM(rows, BF16), dma((1,))],
            heavy,
        )(plan, queries, *got, w, target)

    def place(positions, results, old):
        flat_results = [r for p in positions for r in results[p]]
        fill = old is None
        if fill:
            old = jnp.zeros((8, 128), BF16)
        n = 3 * len(positions) + (slots * blocks if fill else 0)
        return call(
            functools.partial(place_kernel, positions=positions, fill=fill),
            1,
            [ANY] * (len(flat_results) + 1),
            ANY,
            shape(flat, BF16),
            [pltpu.VMEM(rows, BF16), dma((n,))],
            **({} if fill else {"input_output_aliases": {len(flat_results) + 1: 0}}),
        )(plan, *flat_results, old)

    w, m = w0, m0
    results = {}
    got, packed = lax.optimization_barrier((got, packed))
    for p in range(run):
        pair, scale = sums(p, got, 1 if p else 0, w)
        if p < run - 1:
            packed, got, pair = lax.optimization_barrier((packed, got, pair))
            coming = tuple(far(a) for a in both_ways(packed[2 * p], packed[2 * p + 1]))
        parts = lax.all_to_all(pair, "z", 0, 0, tiled=True)
        if p:
            result = answer(p - 1, got, 0, w)
            parts, result = lax.optimization_barrier((parts, result))
            results[p - 1] = (result, *both_ways(result, result))
        chunk, m = update(p, parts, m, scale)
        w = lax.all_gather(chunk, ("z", "core"), axis=0)
        if p < run - 1:
            got = coming
    result = answer(run - 1, got, len(wanted[-1]) - 1, w)
    results[run - 1] = (result, *both_ways(result, result))
    out = place(tuple(range(run - 1)), results, None)
    out = place((run - 1,), results, out)
    return out.reshape(slots, blocks, block_rows, width)


def solution(mesh):
    seq, head, rows = (mesh.shape[name] for name in ("seq", "head", "rows"))
    split = Mesh(mesh.devices.reshape(seq, head, rows // 2, 2), ("seq", "head", "z", "core"))
    data = P("seq", None, ("z", "core"), "head")
    weight = P("head", None, None)
    return jax.shard_map(
        body,
        mesh=split,
        in_specs=(data, data, data, P(), P("head"), weight, weight, weight),
        out_specs=data,
        check_vma=False,
    )
```

```python
import functools

import jax
import jax.numpy as jnp
from jax import lax
from jax.experimental import pallas as pl
from jax.experimental.pallas import tpu as pltpu
from jax.sharding import Mesh, PartitionSpec as P

F32 = jnp.float32
BF16 = jnp.bfloat16
NT = (((1,), (1,)), ((), ()))
NN = (((1,), (0,)), ((), ()))
TN = (((0,), (0,)), ((), ()))


def dot(first_op, second_op, dims):
    return lax.dot_general(first_op, second_op, dims, preferred_element_type=F32)


def normalized(rows, epsilon):
    rows = rows.astype(F32)
    return rows * lax.rsqrt(jnp.mean(rows * rows, axis=-1, keepdims=True) + epsilon)


def weights_of(w_ref, target_ref):
    parts = [w_ref[:, i].reshape(-1, w_ref.shape[3]) for i in range(3)]
    down = parts[2].astype(F32)
    scale = target_ref[...] / jnp.sqrt(jnp.sum(down * down, axis=0, keepdims=True) + 1e-06)
    return parts[0], parts[1], (down * scale).astype(BF16), scale


SOURCE, OWN, RESTART, HIGH, LOW, DEAD, CORE, KEPT = 0, 4, 8, 12, 16, 20, 28, 32
PLAN = 40


def copy_all(pairs, sem):
    copies = [pltpu.make_async_copy(a, b, sem.at[i]) for i, (a, b) in enumerate(pairs)]
    for c in copies:
        c.start()
    return copies


def stage(pairs, stage_ref, sem):
    inward = copy_all([(a, stage_ref.at[i]) for i, (a, _) in enumerate(pairs)], sem)
    outward = []
    for i, (_, b) in enumerate(pairs):
        inward[i].wait()
        outward.append(pltpu.make_async_copy(stage_ref.at[i], b, sem.at[len(pairs) + i]))
        outward[-1].start()
    for c in outward:
        c.wait()


def plan_kernel(counts, k_ref, v_ref, plan, up_ref, down_ref, stage_ref, sem, *, run, slots, blocks):
    group = lax.axis_index("seq")
    n = lax.axis_size("seq") * slots
    ends, total = [], 0
    for s in range(n):
        total = total + counts[s]
        ends.append(total)

    def find(b):
        seq, start = jnp.int32(0), jnp.int32(0)
        for end in ends:
            passed = end <= b
            seq = seq + passed.astype(jnp.int32)
            start = jnp.where(passed, end, start)
        return seq, b - start

    for p in range(run):
        seq, block = find(group * run + p)
        owner = seq // slots
        flat = jnp.clip((seq - owner * slots) * blocks + block, 0, slots * blocks - 1)
        plan[SOURCE + p] = jnp.clip(owner - group + 1, 0, 2)
        plan[OWN + p] = flat
        plan[RESTART + p] = (block == 0).astype(jnp.int32)
        plan[KEPT + p] = jnp.where(owner == group, flat, -1)
        for place, other in ((HIGH, group + 1), (LOW, group - 1)):
            b = other * run + p
            seq, block = find(b)
            flat = jnp.clip((seq - group * slots) * blocks + block, 0, slots * blocks - 1)
            plan[place + p] = jnp.where((b >= 0) & (seq // slots == group), flat, -1)
    for i in range(slots * blocks):
        plan[DEAD + i] = (i % blocks >= counts[group * slots + i // blocks]).astype(jnp.int32)
    plan[CORE] = lax.axis_index("core")
    high, low = jnp.maximum(plan[HIGH], 0), jnp.maximum(plan[LOW], 0)
    pairs = [(k_ref.at[high], up_ref.at[0]), (v_ref.at[high], up_ref.at[1])]
    pairs += [(k_ref.at[low], down_ref.at[0]), (v_ref.at[low], down_ref.at[1])]
    stage(pairs, stage_ref, sem)


def pack_kernel(plan, q_ref, k_ref, v_ref, *refs, wanted):
    stage_ref, sem, outs = refs[-2], refs[-1], refs[:-2]
    pairs = []
    for j, batch in enumerate(wanted):
        for side, place in enumerate((HIGH, LOW)):
            for i, (name, p) in enumerate(batch):
                source = {"q": q_ref, "k": k_ref, "v": v_ref}[name]
                pairs.append((source.at[jnp.maximum(plan[place + p], 0)], outs[2 * j + side].at[i]))
    stage(pairs, stage_ref, sem)


def fetch(plan, p, wanted, sem):
    for s in range(3):

        @pl.when(plan[SOURCE + p] == s)
        def _():
            for i, (local, up, down, at, target) in enumerate(wanted):
                source = (up.at[at], local.at[plan[OWN + p]], down.at[at])[s]
                pltpu.make_async_copy(source, target, sem.at[i]).start()

    return [pltpu.make_async_copy(w[0].at[0], w[4], sem.at[i]) for i, w in enumerate(wanted)]


def init_kernel(gate_hbm, up_hbm, down_hbm, w_ref, m_ref, goal_ref, target_ref, gate_ref, up_ref, down_ref, sem):
    me = lax.axis_index("z") * lax.axis_size("core") + lax.axis_index("core")
    for c in copy_all([(gate_hbm.at[0], gate_ref), (up_hbm.at[0], up_ref), (down_hbm.at[0], down_ref)], sem):
        c.wait()
    n_dev, _, share, width = w_ref.shape
    down = down_ref[...]
    for i, part in enumerate((gate_ref[...].astype(F32).T.astype(BF16), up_ref[...].astype(F32).T.astype(BF16), down)):
        w_ref[:, i] = part.reshape(n_dev, share, width)
    down = down.astype(F32)
    target_ref[...] = jnp.sqrt(jnp.sum(down * down, axis=0, keepdims=True) + 1e-06)
    mine = w_ref[me].astype(F32)
    m_ref[...] = mine
    for i in range(2):
        goal_ref[i] = jnp.sqrt(jnp.sum(mine[i] * mine[i], axis=1, keepdims=True) + 1e-06)


def sums_kernel(plan, k_hbm, v_hbm, up_hbm, down_hbm, w_ref, w0_ref, target_ref, keep_ref, send_ref, scale_ref, k_ref, v_ref, sem, *, p, at):
    copies = fetch(plan, p, [(k_hbm, up_hbm, down_hbm, at, k_ref), (v_hbm, up_hbm, down_hbm, at + 1, v_ref)], sem)
    core = plan[CORE]
    w = jnp.where(plan[RESTART + p] == 1, w0_ref[...], w_ref[...])
    gate, up, down, scale = weights_of(w, target_ref)
    scale_ref[...] = scale
    for c in copies:
        c.wait()
    keys = normalized(k_ref[...], 1e-06).astype(BF16)
    values = v_ref[...]
    gate_pre = dot(keys, gate, NT)
    up_pre = dot(keys, up, NT)
    d_hidden = dot(values, down, NT)
    gate_sig = jax.nn.sigmoid(gate_pre)
    gate_act = gate_pre * gate_sig
    hidden = (gate_act * up_pre).astype(BF16)
    d_gate = (d_hidden * up_pre * gate_sig * (1.0 + gate_pre * (1.0 - gate_sig))).astype(BF16)
    d_up = (d_hidden * gate_act).astype(BF16)
    n, _, rows, width = keep_ref.shape
    for i, (left, right) in enumerate(((d_gate, keys), (d_up, keys), (hidden, values))):
        total = dot(left, right, TN).astype(BF16).reshape(n, 2, rows, width)

        @pl.when(core == 0)
        def _():
            keep_ref[:, i] = total[:, 0]
            send_ref[:, i] = total[:, 1]

        @pl.when(core == 1)
        def _():
            keep_ref[:, i] = total[:, 1]
            send_ref[:, i] = total[:, 0]


def update_kernel(plan, step_ref, x_ref, m_ref, m0_ref, scale_ref, goal_ref, w_ref, out_ref, *, p):
    restart = plan[RESTART + p] == 1
    total = jnp.sum(x_ref[...].astype(F32), axis=0) * step_ref[0]
    for i in range(3):
        old = jnp.where(restart, m0_ref[i], m_ref[i])
        if i == 2:
            new = old * scale_ref[...] + total[i]
        else:
            moved = old + total[i]
            norm = jnp.sqrt(jnp.sum(moved * moved, axis=1, keepdims=True) + 1e-06)
            new = moved * (goal_ref[i] / norm)
        out_ref[i] = new
        w_ref[i] = new.astype(BF16)


def answer_kernel(plan, q_hbm, up_hbm, down_hbm, w_ref, target_ref, out_ref, q_ref, sem, *, p, at):
    copies = fetch(plan, p, [(q_hbm, up_hbm, down_hbm, at, q_ref)], sem)
    gate, up, down, _ = weights_of(w_ref, target_ref)
    for c in copies:
        c.wait()
    query = normalized(q_ref[...], 1e-06).astype(BF16)
    out_gate = dot(query, gate, NT)
    out_up = dot(query, up, NT)
    out_hidden = (out_gate * jax.nn.sigmoid(out_gate) * out_up).astype(BF16)
    out_ref[...] = normalized(dot(out_hidden, down, NN), 1e-05).astype(BF16)


def place_kernel(plan, *refs, positions, fill):
    n = 3 * len(positions)
    old, out_ref, zero_ref, sem = refs[n:]
    moves = []
    for j, p in enumerate(positions):
        for i, place in enumerate((KEPT, LOW, HIGH)):
            moves.append((plan[place + p] >= 0, refs[3 * j + i], jnp.maximum(plan[place + p], 0)))
    if fill:
        zero_ref[...] = jnp.zeros_like(zero_ref)
        moves += [(plan[DEAD + i] == 1, zero_ref, i) for i in range(out_ref.shape[0])]
    copies = [(on, pltpu.make_async_copy(source, out_ref.at[i], sem.at[k])) for k, (on, source, i) in enumerate(moves)]
    for on, c in copies:
        pl.when(on)(c.start)
    for on, c in copies:
        pl.when(on)(c.wait)


def call(kernel, n_scalars, in_specs, out_specs, out_shape, scratch=(), cost=None, **kw):
    return pl.pallas_call(
        kernel,
        grid_spec=pltpu.PrefetchScalarGridSpec(
            num_scalar_prefetch=n_scalars, grid=(1,), in_specs=in_specs, out_specs=out_specs, scratch_shapes=scratch
        ),
        out_shape=out_shape,
        compiler_params=pltpu.CompilerParams(vmem_limit_bytes=16 << 20),
        cost_estimate=cost,
        **kw,
    )


def whole(shape):
    return pl.BlockSpec(shape, lambda *_: (0,) * len(shape))


ANY = pl.BlockSpec(memory_space=pl.ANY)
HBM = pl.BlockSpec(memory_space=pltpu.HBM)
VMEM = pl.BlockSpec(memory_space=pltpu.VMEM)


def body(queries, keys, values, counts, rate, w_first, w_third, w_second):
    slots, blocks, block_rows, width = queries.shape
    hidden = w_first.shape[2]
    n_z, n_core, n_seq = lax.axis_size("z"), lax.axis_size("core"), lax.axis_size("seq")
    n_dev = n_z * n_core
    share = hidden // n_dev
    run = blocks
    step = (rate / (block_rows * n_dev)).astype(F32)
    rows = (block_rows, width)
    flat = (slots * blocks, *rows)
    far = lambda a: pltpu.with_memory_space_constraint(a, pltpu.HBM)
    queries, keys, values = (far(a.reshape(flat)) for a in (queries, keys, values))
    w_shape, half, m_shape = (n_dev, 3, share, width), (n_z, 3, share, width), (3, share, width)
    goal_shape, line = (2, share, 1), (1, width)
    shape = jax.ShapeDtypeStruct
    dma = pltpu.SemaphoreType.DMA
    heavy = pl.CostEstimate(flops=2 * 3 * 2 * block_rows * width * hidden, transcendentals=0, bytes_accessed=6 << 20)

    def both_ways(up, down):
        upward = [(i, i + 1) for i in range(n_seq - 1)]
        return lax.ppermute(up, "seq", upward), lax.ppermute(down, "seq", [(b, a) for a, b in upward])

    def batch_shape(n):
        return pltpu.HBM((n, *rows), BF16)

    plan, up, down = call(
        functools.partial(plan_kernel, run=run, slots=slots, blocks=blocks),
        1,
        [HBM, HBM],
        [pl.BlockSpec(memory_space=pltpu.SMEM), HBM, HBM],
        [shape((PLAN,), jnp.int32), batch_shape(2), batch_shape(2)],
        [pltpu.VMEM((4, *rows), BF16), dma((8,))],
    )(counts, keys, values)
    got = both_ways(up, down)

    wanted = [[("q", p - 1), ("k", p), ("v", p)] for p in range(1, run)]
    wanted[-1].append(("q", run - 1))

    sizes = [len(b) for b in wanted for _ in range(2)]
    packed = call(
        functools.partial(pack_kernel, wanted=wanted),
        1,
        [HBM, HBM, HBM],
        [HBM] * len(sizes),
        [batch_shape(n) for n in sizes],
        [pltpu.VMEM((sum(sizes), *rows), BF16), dma((2 * sum(sizes),))],
    )(plan, queries, keys, values)

    w0, m0, goal, target = call(
        init_kernel,
        0,
        [HBM, HBM, HBM],
        [whole(w_shape), whole(m_shape), whole(goal_shape), whole(line)],
        [shape(w_shape, BF16), shape(m_shape, F32), shape(goal_shape, F32), shape(line, F32)],
        [pltpu.VMEM((width, hidden), BF16), pltpu.VMEM((width, hidden), BF16), pltpu.VMEM((hidden, width), BF16), dma((3,))],
    )(w_first, w_third, w_second)

    def sums(p, got, at, w):
        keep, send, scale = call(
            functools.partial(sums_kernel, p=p, at=at),
            1,
            [HBM, HBM, ANY, ANY, whole(w_shape), whole(w_shape), whole(line)],
            [whole(half), whole(half), whole(line)],
            [shape(half, BF16), shape(half, BF16), shape(line, F32)],
            [pltpu.VMEM(rows, BF16), pltpu.VMEM(rows, BF16), dma((2,))],
            heavy,
        )(plan, keys, values, *got, w, w0, target)
        other = lax.ppermute(send, "core", [(0, 1), (1, 0)])
        return (keep.astype(F32) + other.astype(F32)).astype(BF16), scale

    def update(p, x, m, scale):
        return call(
            functools.partial(update_kernel, p=p),
            2,
            [whole(half), whole(m_shape), whole(m_shape), whole(line), whole(goal_shape)],
            [whole(m_shape), whole(m_shape)],
            [shape(m_shape, BF16), shape(m_shape, F32)],
        )(plan, step, x, m, m0, scale, goal)

    def answer(p, got, at, w):
        return call(
            functools.partial(answer_kernel, p=p, at=at),
            1,
            [HBM, ANY, ANY, whole(w_shape), whole(line)],
            whole(rows),
            shape(rows, BF16),
            [pltpu.VMEM(rows, BF16), dma((1,))],
            heavy,
        )(plan, queries, *got, w, target)

    def place(positions, results, old):
        flat_results = [r for p in positions for r in results[p]]
        fill = old is None
        if fill:
            old = queries
        n = 3 * len(positions) + (slots * blocks if fill else 0)
        return call(
            functools.partial(place_kernel, positions=positions, fill=fill),
            1,
            [VMEM] * len(flat_results) + [HBM],
            HBM,
            pltpu.HBM(flat, BF16),
            [pltpu.VMEM(rows, BF16), dma((n,))],
            **({} if fill else {"input_output_aliases": {len(flat_results) + 1: 0}}),
        )(plan, *flat_results, old)

    w, m = w0, m0
    results = {}
    got, packed = lax.optimization_barrier((got, packed))
    for p in range(run):
        pair, scale = sums(p, got, 1 if p else 0, w)
        if p < run - 1:
            packed, got, pair = lax.optimization_barrier((packed, got, pair))
            coming = tuple(far(a) for a in both_ways(packed[2 * p], packed[2 * p + 1]))
        parts = lax.all_to_all(pair, "z", 0, 0, tiled=True)
        if p:
            result = answer(p - 1, got, 0, w)
            parts, _ = lax.optimization_barrier((parts, result))
            results[p - 1] = (result, *both_ways(result, result))
        chunk, m = update(p, parts, m, scale)
        w = lax.all_gather(chunk, ("z", "core"), axis=0)
        if p < run - 1:
            got = coming
    result = answer(run - 1, got, len(wanted[-1]) - 1, w)
    results[run - 1] = (result, *both_ways(result, result))
    out = place(tuple(range(run - 1)), results, None)
    out = place((run - 1,), results, out)
    return out.reshape(slots, blocks, block_rows, width)


def solution(mesh):
    seq, head, rows = (mesh.shape[name] for name in ("seq", "head", "rows"))
    split = Mesh(mesh.devices.reshape(seq, head, rows // 2, 2), ("seq", "head", "z", "core"))
    data = P("seq", None, ("z", "core"), "head")
    weight = P("head", None, None)
    return jax.shard_map(
        body,
        mesh=split,
        in_specs=(data, data, data, P(), P("head"), weight, weight, weight),
        out_specs=data,
        check_vma=False,
    )
```
